32 devices in a mesh: lat: 2 (over core), prop: 16 (over z, y, x).
Axes of the slice: x: 2, y: 2, z: 4, core: 2. Of those that a mesh axis runs over, the one named last changes fastest.
Arguments:
- right_side: float32 [2, 3, 16, 64, 4, 128], P(None, None, None, 'prop', 'lat'), may hold values from -30 to 30
- start_field: float32 [2, 3, 16, 64, 4, 128], P(None, None, None, 'prop', 'lat'), may hold values from -1.75 to 1.75
- region: int32 [64, 4, 128], P('prop', 'lat'), may hold values from 0 to 7
- core_mask: int32 [64, 4, 128], P('prop', 'lat'), may hold values 0 or 1
- intensity: float32 [64, 4, 128], P('prop', 'lat'), may hold values from 0 to 4
- eps_lin: float32 [8], replicated, may hold values from 1 to 12
- eps_loss: float32 [8], replicated, may hold values from 0.1 to 3
- kerr_coef: float32 [8], replicated, may hold values from 0.2 to 1
Outputs:
- new_field: float32 [2, 3, 16, 64, 4, 128], P(None, None, None, 'prop', 'lat')
The draws below stay inside these ranges and needn't reach their ends.
All inputs are finite; a program needn't handle non-finite values. No bound on the sum of `core_mask` on one device may be relied on, other than what follows from the above.
Results may differ from the reference program's by a relative error of at most 0.00002.
Values sent between devices are 32-bit elements; how exact they have to be, the bound alone decides.
A program may use at most 64 MiB of HBM per device.

```python
import math
import jax
import jax.numpy as jnp
from jax import lax

S = 16
NY = 128
NREG = 8
NZ = 64
NX = 4


def draw_right_side(key, part):
    first_key, second_key = jax.random.split(jax.random.fold_in(key, 7))
    full_shape = (2, 3, S, NZ, NX, NY)
    z_fraction = jnp.arange(NZ, dtype=jnp.float32) / max(NZ - 1, 1)
    profile = (1.0 + 2.0 * z_fraction)[:, None, None]
    lateral = jnp.exp(jax.random.uniform(second_key, (NX, NY), jnp.float32, 0.0, math.log(10.0 / 3.0)))
    noise = jnp.clip(jax.random.normal(first_key, full_shape, jnp.float32), -3.0, 3.0)
    return (noise * profile * lateral).astype(jnp.float32)


def with_ends(drawn, own_key, low, largest):
    dims = drawn.shape
    place = [jax.random.randint(jax.random.fold_in(own_key, axis), (), 0, dims[axis]) for axis in range(len(dims))]
    drawn = drawn.at[tuple(place)].set(low)
    longest = dims.index(max(dims))
    place[longest] = (place[longest] + 1) % dims[longest]
    return drawn.at[tuple(place)].set(largest)


def levels(key, extent, cuts, low, top_value):
    def one(dim, parts):
        heights = jax.random.uniform(jax.random.fold_in(jax.random.fold_in(key, 6), dim), (parts,), jnp.float32, low / len(cuts), top_value / len(cuts))
        return jnp.repeat(jnp.exp(heights), extent[dim] // parts).reshape((-1,) + (1,) * (len(extent) - dim - 1))

    level = one(*cuts[0])
    for cut in cuts[1:]:
        level = level * one(*cut)
    return level


def gaussian(own_key, shape, scale, reach, cuts=(), kind=jnp.bfloat16):
    factor_of = levels(own_key, shape, cuts, -0.22, 0.18) if cuts else 1.0
    drawn = jax.random.normal(own_key, shape, jnp.float32) * scale * factor_of
    return jnp.minimum(jnp.maximum(drawn, -reach), reach).astype(kind)


def setup_inputs(seed: int = 0) -> dict:
    key_of = jax.random.split(jax.random.key(seed), 9)
    right_side = draw_right_side(jax.random.fold_in(key_of[8], 71), 0)
    start_field = gaussian(key_of[1], (2, 3, S, NZ, NX, NY), 0.3, 1.75, ((3, 16), (4, 2)), jnp.float32)
    region = with_ends(jax.random.randint(key_of[2], (NZ, NX, NY), 0, NREG), jax.random.fold_in(key_of[2], 1), 0, NREG - 1).astype(jnp.int32)
    core_mask = with_ends((jax.random.randint(key_of[3], (NZ, NX, NY), 0, 3) < 1).astype(jnp.int32), jax.random.fold_in(key_of[3], 1), 0, 1)
    intensity = jnp.clip(4.0 * jax.random.uniform(key_of[4], (NZ, NX, NY), jnp.float32) ** levels(key_of[4], (NZ, NX, NY), ((0, 16), (1, 2)), -0.2, 0.2), 0.0, 4.0)
    eps_lin = jnp.clip(jax.random.uniform(key_of[5], (NREG,), jnp.float32, 1.0, 12.0), 1.0, 12.0)
    eps_loss = jnp.clip(jnp.exp(jax.random.uniform(key_of[6], (NREG,), jnp.float32, math.log(0.1), math.log(3.0))), 0.1, 3.0)
    kerr_coef = jnp.clip(jax.random.uniform(key_of[7], (NREG,), jnp.float32, 0.2, 1.0), 0.2, 1.0)
    return dict(right_side=right_side, start_field=start_field, region=region, core_mask=core_mask, intensity=intensity, eps_lin=eps_lin, eps_loss=eps_loss, kerr_coef=kerr_coef)


wave_sq = 0.25
wave_shift = 0.02
loss_gain = 3.2
tiny = 1e-6


def trimmed(values, direction):
    selector = [slice(None)] * (values.ndim - 3) + [slice(0, -1)] * 3
    if direction is not None:
        selector[values.ndim + direction] = slice(1, None)
    return values[tuple(selector)]


def advance(values, direction):
    return trimmed(values, direction) - trimmed(values, None)


def upper(values, direction):
    selector = [slice(None)] * (values.ndim - 3) + [slice(1, None)] * 3
    if direction is not None:
        selector[values.ndim + direction] = slice(0, -1)
    return values[tuple(selector)]


def retreat(values, direction):
    return upper(values, None) - upper(values, direction)


def curl_twice(padded):
    field_x = padded[:, 0]
    field_y = padded[:, 1]
    field_z = padded[:, 2]
    magnet_x = advance(field_z, -1) - advance(field_y, -3)
    magnet_y = advance(field_x, -3) - advance(field_z, -2)
    magnet_z = advance(field_y, -2) - advance(field_x, -1)
    result_x = retreat(magnet_z, -1) - retreat(magnet_y, -3)
    result_y = retreat(magnet_x, -3) - retreat(magnet_z, -2)
    result_z = retreat(magnet_y, -2) - retreat(magnet_x, -1)
    return jnp.stack([result_x, result_y, result_z], axis=1)


def apply_operator(values, padded, perm_real, perm_imag):
    curled = curl_twice(padded)
    real_part = values[0]
    imag_part = values[1]
    out_real = curled[0] - wave_sq * (perm_real * real_part - perm_imag * imag_part)
    out_imag = curled[1] - wave_sq * (perm_real * imag_part + perm_imag * real_part)
    return jnp.stack([out_real, out_imag])


def descend(gain_real, gain_imag, previous, plane_real, plane_imag, source):
    denom_real = plane_real - gain_real
    denom_imag = plane_imag - gain_imag
    magnitude = denom_real * denom_real + denom_imag * denom_imag
    new_real = denom_real / magnitude
    new_imag = -denom_imag / magnitude
    sum_real = source[0] + previous[0]
    sum_imag = source[1] + previous[1]
    updated = jnp.stack([new_real * sum_real - new_imag * sum_imag, new_real * sum_imag + new_imag * sum_real])
    return new_real, new_imag, updated


def ascend(gain_real, gain_imag, forward_value, behind):
    return jnp.stack([forward_value[0] + gain_real * behind[0] - gain_imag * behind[1],
                      forward_value[1] + gain_real * behind[1] + gain_imag * behind[0]])


def solve_lines(right_part, diag_real, diag_imag, unroll_count):
    along_first = jnp.moveaxis(right_part, -3, 0)
    diag_rows_real = jnp.moveaxis(diag_real, -3, 0)
    diag_rows_imag = jnp.moveaxis(diag_imag, -3, 0)

    def downward(carried, element):
        gain_real, gain_imag, previous = carried
        plane_real, plane_imag, source = element
        gain_real, gain_imag, previous = descend(gain_real, gain_imag, previous, plane_real, plane_imag, source)
        return (gain_real, gain_imag, previous), (gain_real, gain_imag, previous)

    initial = (jnp.zeros_like(diag_rows_real[0]), jnp.zeros_like(diag_rows_real[0]), jnp.zeros_like(along_first[0]))
    unused, (gains_real, gains_imag, fronts) = lax.scan(downward, initial, (diag_rows_real, diag_rows_imag, along_first), unroll=unroll_count)

    def upward(behind, element):
        gain_real, gain_imag, forward_value = element
        new_value = ascend(gain_real, gain_imag, forward_value, behind)
        return new_value, new_value

    unused, values = lax.scan(upward, jnp.zeros_like(along_first[0]), (gains_real, gains_imag, fronts), reverse=True, unroll=unroll_count)
    return jnp.moveaxis(values, 0, -3)


def pad_grid(values):
    return jnp.pad(values, [(0, 0)] * (values.ndim - 3) + [(1, 1)] * 3)


def reference(right_side, start_field, region, core_mask, intensity, eps_lin, eps_loss, kerr_coef):
    perm_real = eps_lin[region] + core_mask.astype(jnp.float32) * kerr_coef[region] * intensity
    perm_imag = eps_loss[region]
    diag_real = 2.0 - wave_shift * perm_real
    diag_imag = (loss_gain / NZ) * perm_imag

    def solve_column(columns):
        right_part, initial = columns
        residual = right_part - apply_operator(initial, pad_grid(initial), perm_real, perm_imag)
        precond = solve_lines(residual, diag_real, diag_imag, 1)
        image_field = apply_operator(precond, pad_grid(precond), perm_real, perm_imag)
        cross_sum = jnp.sum(residual * image_field)
        self_sum = jnp.sum(image_field * image_field)
        return initial + (cross_sum / (self_sum + tiny)) * precond

    updated = lax.map(solve_column, (jnp.moveaxis(right_side, 2, 0), jnp.moveaxis(start_field, 2, 0)))
    return jnp.moveaxis(updated, 0, 2)
```

```python
import functools

import jax
import jax.numpy as jnp
from jax import lax
from jax.experimental import pallas as pl
from jax.experimental.pallas import tpu as pltpu
from jax.sharding import PartitionSpec as P

MESH = pl.DeviceIdType.MESH
wave_sq = 0.25
wave_shift = 0.02
loss_gain = 3.2
tiny = 1e-06


def cmul(a, b):
    return (a[0] * b[0] - a[1] * b[1], a[0] * b[1] + a[1] * b[0])


def cadd(a, b):
    return (a[0] + b[0], a[1] + b[1])


def cinv(a):
    scale = 1.0 / (a[0] * a[0] + a[1] * a[1])
    return (a[0] * scale, -a[1] * scale)


def kernel(
    dims, lin_ref, loss_ref, kerr_ref, region_ref, mask_ref, inten_ref, rhs_ref, start_ref, out_ref,
    field, resid, local, pre, cell, corner, corner_all, link, tips_out, tips_in, ends_out, ends_in, part,
    lat_parts, prop_parts,
    halo_send, halo_recv, corner_send, corner_recv, tips_send, tips_recv, ends_send, ends_recv,
    pre_send, pre_recv, lat_send, lat_recv, prop_send, prop_recv,
):
    n, nl, S, Z, X, NY, u, m, rows = dims
    NREG = lin_ref.shape[0]
    lat = lax.axis_index("lat")
    prop = lax.axis_index("prop")
    has_up, has_down = prop + 1 < n, prop > 0
    has_right, has_left = lat + 1 < nl, lat > 0
    ZX = Z * X

    def at_prop(q):
        return {"lat": lat, "prop": q}

    def at(l, q):
        return {"lat": l, "prop": q}

    def others(count, me, act):
        def body(j, carry):
            act(lax.rem(me + j, count))
            return carry

        lax.fori_loop(1, count, body, 0)

    barrier = pltpu.get_barrier_semaphore()

    def greet(l, q):
        pl.semaphore_signal(barrier, inc=1, device_id=at(l, q), device_id_type=MESH)

    diag_up = jnp.logical_and(has_left, has_up)
    diag_down = jnp.logical_and(has_right, has_down)
    others(n, prop, lambda q: greet(lat, q))
    others(nl, lat, lambda l: greet(l, prop))
    pl.when(diag_up)(lambda: greet(lat - 1, prop + 1))
    pl.when(diag_down)(lambda: greet(lat + 1, prop - 1))

    zero_plane = jnp.zeros((X, S, NY), jnp.float32)
    zero_line = jnp.zeros((S, NY), jnp.float32)
    for c in range(2):
        for k in range(3):
            for z in range(Z):
                for x in range(X):
                    base = (c * 3 + k) * S * ZX + z * X + x
                    field[c, k, z + 1, x + 1] = start_ref[pl.ds(base, S, stride=ZX), :]

    def clear(cond, buf, planes, xs):
        @pl.when(cond)
        def _():
            for c in range(2):
                for k in range(3):
                    for z in planes:
                        for x in xs:
                            buf[c, k, z, x] = zero_line

    no_up, no_down = jnp.logical_not(has_up), jnp.logical_not(has_down)
    no_right, no_left = jnp.logical_not(has_right), jnp.logical_not(has_left)
    inner_z, inner_x = range(1, Z + 1), range(1, X + 1)
    for buf, wide in ((field, inner_z), (pre, range(Z + 2))):
        clear(no_left, buf, wide, (0,))
        clear(no_right, buf, wide, (X + 1,))
    clear(no_down, field, (0,), inner_x)
    clear(no_up, field, (Z + 1,), inner_x)
    clear(jnp.logical_or(no_down, no_right), field, (0,), (X + 1,))
    clear(jnp.logical_or(no_up, no_left), field, (Z + 1,), (0,))

    region = region_ref[...]
    lin = jnp.zeros((Z, X, NY), jnp.float32)
    loss = lin
    kerr = lin
    for r in range(NREG):
        hit = region == r
        lin = jnp.where(hit, lin_ref[r], lin)
        loss = jnp.where(hit, loss_ref[r], loss)
        kerr = jnp.where(hit, kerr_ref[r], kerr)
    perm_real = lin + mask_ref[...].astype(jnp.float32) * kerr * inten_ref[...]
    diag_real = 2.0 - wave_shift * perm_real
    diag_imag = loss_gain / (Z * n) * loss
    gains = []
    for z in range(Z):
        d = (diag_real[z], diag_imag[z])
        if z:
            d = (d[0] - gains[-1][0], d[1] - gains[-1][1])
        gains.append(cinv(d))
    front = [gains[0]]
    for z in range(1, Z):
        front.append(cmul(gains[z], front[-1]))
    from_below = [front[-1]]
    from_above = [gains[-1]]
    for z in range(Z - 2, -1, -1):
        from_below.insert(0, cadd(front[z], cmul(gains[z], from_below[0])))
        from_above.insert(0, cmul(gains[z], from_above[0]))
    for z in range(Z):
        kinds = (wave_sq * perm_real[z], wave_sq * loss[z], *gains[z], *from_below[z], *from_above[z])
        for i, value in enumerate(kinds):
            for x in range(X):
                cell[i, z, x] = value[x : x + 1, :]
    triple = (*from_below[0], *from_below[-1], *from_above[-1])
    for x in range(X):
        for i, value in enumerate(triple):
            corner[x, i : i + 1, :] = value[x : x + 1, :]
        corner[x, 6:8, :] = jnp.zeros((2, NY), jnp.float32)

    count = (n - 1) + (nl - 1) + diag_up.astype(jnp.int32) + diag_down.astype(jnp.int32)
    pl.semaphore_wait(barrier, count)

    def remote(src, dst, send, recv, device):
        return pltpu.make_async_remote_copy(
            src_ref=src, dst_ref=dst, send_sem=send, recv_sem=recv, device_id=device, device_id_type=MESH
        )

    iz, ix = pl.ds(1, Z), pl.ds(1, X)
    halo = [
        (has_up, field.at[:, :, Z, ix], field.at[:, :, 0, ix], at(lat, prop + 1), has_down),
        (has_down, field.at[:, 0:2, 1, ix], field.at[:, 0:2, Z + 1, ix], at(lat, prop - 1), has_up),
        (diag_up, field.at[:, 2, Z, 1], field.at[:, 2, 0, X + 1], at(lat - 1, prop + 1), diag_down),
        (diag_down, field.at[:, 0, 1, X], field.at[:, 0, Z + 1, 0], at(lat + 1, prop - 1), diag_up),
        (has_right, field.at[:, :, iz, X], field.at[:, :, iz, 0], at(lat + 1, prop), has_left),
        (has_left, field.at[:, 1:3, iz, 1], field.at[:, 1:3, iz, X + 1], at(lat - 1, prop), has_right),
    ]
    halos = [
        (remote(src, dst, halo_send.at[i], halo_recv.at[i], device), out, into)
        for i, (out, src, dst, device, into) in enumerate(halo)
    ]
    for copy, out, _ in halos:
        pl.when(out)(copy.start)

    def corner_copy(q):
        return remote(corner.at[q // m], corner_all.at[prop], corner_send.at[q], corner_recv.at[prop], at_prop(q))

    others(n, prop, lambda q: corner_copy(q).start())
    corner_all[prop] = corner[prop // m]

    lane = lax.broadcasted_iota(jnp.int32, (X, S, NY), 2)
    at_first, at_last = lane == 0, lane == NY - 1

    def after(v):
        return jnp.where(at_last, 0.0, pltpu.roll(v, NY - 1, 2))

    def before(v):
        return jnp.where(at_first, 0.0, pltpu.roll(v, 1, 2))

    def curl(buf, c, z):
        def get(k, dz, dx):
            return buf[c, k, z + 1 + dz, 1 + dx : 1 + dx + X]

        ux, uy, uz = get(0, 0, 0), get(1, 0, 0), get(2, 0, 0)
        ux_up, uy_up = get(0, 1, 0), get(1, 1, 0)
        uz_down = get(2, -1, 0)
        uy_right, uz_right = get(1, 0, 1), get(2, 0, 1)
        ux_left = get(0, 0, -1)
        t = uy_right - uy
        out_x = (
            t + 4.0 * ux - after(ux) - before(ux + t) - get(0, -1, 0) - ux_up
            + (uz_right - uz) - (get(2, -1, 1) - uz_down)
        )
        ab = (uz - uz_down) + (ux - ux_left)
        out_y = 4.0 * uy - get(1, -1, 0) - uy_up - get(1, 0, -1) - uy_right + after(ab) - ab
        e = uy_up - uy
        out_z = (
            e + 4.0 * uz - after(uz) - before(uz + e) - get(2, 0, -1) - uz_right
            + (ux_up - ux) - (get(0, 1, -1) - ux_left)
        )
        return (out_x, out_y, out_z), (ux, uy, uz)

    def operate(buf, z):
        pr, pi = cell[0, z], cell[1, z]
        curl_re, re = curl(buf, 0, z)
        curl_im, im = curl(buf, 1, z)
        out_re = [curl_re[k] - (pr * re[k] - pi * im[k]) for k in range(3)]
        out_im = [curl_im[k] - (pr * im[k] + pi * re[k]) for k in range(3)]
        return out_re, out_im

    def residual(z):
        for c, parts in enumerate(operate(field, z)):
            for k in range(3):
                for x in range(X):
                    base = (c * 3 + k) * S * ZX + z * X + x
                    resid[c, k, z, x] = rhs_ref[pl.ds(base, S, stride=ZX), :] - parts[k][x]

    for i in (4, 5):
        pl.when(halos[i][2])(halos[i][0].wait_recv)
    for z in range(1, Z - 1):
        residual(z)
    for i in (0, 2):
        pl.when(halos[i][2])(halos[i][0].wait_recv)
    residual(0)
    for i in (1, 3):
        pl.when(halos[i][2])(halos[i][0].wait_recv)
    if Z > 1:
        residual(Z - 1)

    def coef(i, z):
        return (cell[i, z], cell[i + 1, z])

    def slot(base, b, c, k, a):
        return base + ((b * 2 + c) * 3 + k) * u + a

    for k in range(3):
        held = None
        for z in range(Z):
            r = (resid[0, k, z], resid[1, k, z])
            if held is not None:
                r = cadd(r, held)
            held = cmul(coef(2, z), r)
            if z < Z - 1:
                local[0, k, z] = held[0]
                local[1, k, z] = held[1]
        local[0, k, Z - 1], local[1, k, Z - 1] = held
        last = held
        for z in range(Z - 2, -1, -1):
            held = cadd((local[0, k, z], local[1, k, z]), cmul(coef(2, z), held))
            local[0, k, z], local[1, k, z] = held
        for b, ends in enumerate((held, last)):
            for c in range(2):
                for x in range(X):
                    for a in range(u):
                        tips_out[pl.ds(slot(x * m * rows, b, c, k, a), m, stride=rows), :] = ends[c][x, a * m : (a + 1) * m]

    def block(q):
        return pl.ds(pl.multiple_of(q * rows, 8), rows)

    def tips_copy(q):
        return remote(tips_out.at[block(q)], tips_in.at[block(prop)], tips_send.at[q], tips_recv.at[prop], at_prop(q))

    others(n, prop, lambda q: tips_copy(q).start())
    tips_in[block(prop), :] = tips_out[block(prop), :]

    def corner_from(q):
        return remote(corner.at[q // m], corner_all.at[q], corner_send.at[q], corner_recv.at[q], at_prop(q))

    others(n, prop, lambda q: corner_from(q).wait_recv())
    beta = (jnp.zeros((1, NY), jnp.float32),) * 2

    def link_step(k, beta):
        first, cross, last = [(corner_all[k, 2 * i : 2 * i + 1, :], corner_all[k, 2 * i + 1 : 2 * i + 2, :]) for i in range(3)]
        fb = cmul(first, beta)
        gamma = cinv((1.0 - fb[0], -fb[1]))
        carry = cmul(cross, gamma)
        mix = cmul(carry, beta)
        for i, value in enumerate((*carry, *mix, *gamma, *cmul(gamma, first), *beta)):
            link[k, i] = value
        return cadd(last, cmul(cross, mix))

    for k in range(n):
        beta = link_step(k, beta)

    def tips_from(q):
        return remote(tips_out.at[block(q)], tips_in.at[block(q)], tips_send.at[q], tips_recv.at[q], at_prop(q))

    others(n, prop, lambda q: tips_from(q).wait_recv())
    span = 3 * u

    def linked(k, i):
        return (link[k, 2 * i], link[k, 2 * i + 1])

    def tip(k, b):
        return tuple(tips_in[k * rows + (b * 2 + c) * span : k * rows + (b * 2 + c + 1) * span, :] for c in range(2))

    def put(k, b, value):
        for c in range(2):
            ends_out[k * rows + (b * 2 + c) * span : k * rows + (b * 2 + c + 1) * span, :] = value[c]

    none = (jnp.zeros((span, NY), jnp.float32),) * 2
    alphas = [none]
    for k in range(n):
        alphas.append(
            cadd(cadd(tip(k, 1), cmul(linked(k, 1), tip(k, 0))), cmul(linked(k, 0), alphas[-1]))
        )
    first = none
    for k in range(n - 1, -1, -1):
        put(k, 1, first)
        source = cadd(cmul(linked(k, 2), tip(k, 0)), cmul(linked(k, 3), alphas[k]))
        first = cadd(source, cmul(linked(k, 0), first))
        put(k, 0, cadd(alphas[k], cmul(linked(k, 4), first)) if k else none)

    def ends_copy(q):
        return remote(ends_out.at[block(q)], ends_in.at[block(prop)], ends_send.at[q], ends_recv.at[prop], at_prop(q))

    def ends_from(q):
        return remote(ends_out.at[block(q)], ends_in.at[block(q)], ends_send.at[q], ends_recv.at[q], at_prop(q))

    others(n, prop, lambda q: ends_copy(q).start())
    ends_in[block(prop), :] = ends_out[block(prop), :]
    others(n, prop, lambda q: ends_from(q).wait_recv())

    for k in range(3):
        sides = []
        for b in range(2):
            for c in range(2):
                for x in range(X):
                    for a in range(u):
                        pre[c, k, b * (Z + 1), 1 + x, a * m : (a + 1) * m, :] = ends_in[
                            pl.ds(slot(x * m * rows, b, c, k, a), m, stride=rows), :
                        ]
            sides.append(tuple(pre[c, k, b * (Z + 1), 1 : 1 + X] for c in range(2)))
        for z in range(Z):
            value = cadd((local[0, k, z], local[1, k, z]), cadd(cmul(coef(4, z), sides[0]), cmul(coef(6, z), sides[1])))
            for c in range(2):
                pre[c, k, z + 1, 1 : 1 + X] = value[c]
    side = [
        (has_right, pre.at[:, :, pl.ds(1, Z + 1), X], pre.at[:, :, pl.ds(1, Z + 1), 0], at(lat + 1, prop), has_left),
        (has_left, pre.at[:, 1:3, pl.ds(0, Z + 1), 1], pre.at[:, 1:3, pl.ds(0, Z + 1), X + 1], at(lat - 1, prop), has_right),
    ]
    sides = [
        (remote(src, dst, pre_send.at[i], pre_recv.at[i], device), out, into)
        for i, (out, src, dst, device, into) in enumerate(side)
    ]
    for copy, out, _ in sides:
        pl.when(out)(copy.start)
    for copy, _, into in sides:
        pl.when(into)(copy.wait_recv)

    cross_sum = zero_plane
    self_sum = zero_plane
    for z in range(Z):
        for c, parts in enumerate(operate(pre, z)):
            for k in range(3):
                cross_sum = cross_sum + resid[c, k, z] * parts[k]
                self_sum = self_sum + parts[k] * parts[k]
    column = lax.broadcasted_iota(jnp.int32, (S, NY), 0)
    place = lax.broadcasted_iota(jnp.int32, (S, NY), 1)
    on_cross, on_self = place == column, place == column + S
    totals = [jnp.sum(jnp.sum(v, axis=0), axis=1, keepdims=True) for v in (cross_sum, self_sum)]
    packed = jnp.where(on_cross, totals[0], jnp.where(on_self, totals[1], 0.0))
    row = jnp.sum(packed, axis=0, keepdims=True)

    def reduced(row, count, me, parts, i, send, recv, device):
        part[i] = row
        parts[me] = row

        def copy(q, own):
            return remote(part.at[i], parts.at[own], send.at[q], recv.at[own], device(q))

        others(count, me, lambda q: copy(q, me).start())
        others(count, me, lambda q: copy(q, q).wait_recv())
        others(count, me, lambda q: copy(q, q).wait_send())
        total = parts[0]
        for j in range(1, count):
            total = total + parts[j]
        return total

    row = reduced(row, nl, lat, lat_parts, 0, lat_send, lat_recv, lambda l: at(l, prop))
    row = reduced(row, n, prop, prop_parts, 1, prop_send, prop_recv, at_prop)
    wide = jnp.broadcast_to(row, (S, NY))
    cross_total = jnp.sum(jnp.where(on_cross, wide, 0.0), axis=1, keepdims=True)
    self_total = jnp.sum(jnp.where(on_self, wide, 0.0), axis=1, keepdims=True)
    size = jnp.broadcast_to(cross_total / (self_total + tiny), (S, NY))
    for c in range(2):
        for k in range(3):
            for z in range(Z):
                for x in range(X):
                    base = (c * 3 + k) * S * ZX + z * X + x
                    out_ref[pl.ds(base, S, stride=ZX), :] = field[c, k, z + 1, x + 1] + size * pre[c, k, z + 1, x + 1]
    for copy, out, _ in halos + sides:
        pl.when(out)(copy.wait_send)
    others(n, prop, lambda q: corner_from(q).wait_send())
    others(n, prop, lambda q: tips_from(q).wait_send())
    others(n, prop, lambda q: ends_from(q).wait_send())


def per_device(n, nl, right_side, start_field, region, core_mask, intensity, eps_lin, eps_loss, kerr_coef):
    S, Z, X, NY = right_side.shape[2:]
    m = n // X
    u = S // m
    rows = -(-12 * u // 8) * 8
    dims = (n, nl, S, Z, X, NY, u, m, rows)
    flat = (6 * S * Z * X, NY)
    f32 = jnp.float32
    vmem = pl.BlockSpec(memory_space=pltpu.VMEM)
    smem = pl.BlockSpec(memory_space=pltpu.SMEM)
    dma = pltpu.SemaphoreType.DMA
    out = pl.pallas_call(
        functools.partial(kernel, dims),
        out_shape=jax.ShapeDtypeStruct(flat, f32),
        in_specs=[smem] * 3 + [vmem] * 5,
        out_specs=vmem,
        scratch_shapes=[
            pltpu.VMEM((2, 3, Z + 2, X + 2, S, NY), f32),
            pltpu.VMEM((2, 3, Z, X, S, NY), f32),
            pltpu.VMEM((2, 3, Z, X, S, NY), f32),
            pltpu.VMEM((2, 3, Z + 2, X + 2, S, NY), f32),
            pltpu.VMEM((8, Z, X, 1, NY), f32),
            pltpu.VMEM((X, 8, NY), f32),
            pltpu.VMEM((n, 8, NY), f32),
            pltpu.VMEM((n, 10, 1, NY), f32),
            pltpu.VMEM((n * rows, NY), f32),
            pltpu.VMEM((n * rows, NY), f32),
            pltpu.VMEM((n * rows, NY), f32),
            pltpu.VMEM((n * rows, NY), f32),
            pltpu.VMEM((2, 1, NY), f32),
            pltpu.VMEM((nl, 1, NY), f32),
            pltpu.VMEM((n, 1, NY), f32),
            dma((6,)), dma((6,)),
            dma((n,)), dma((n,)),
            dma((n,)), dma((n,)),
            dma((n,)), dma((n,)),
            dma((2,)), dma((2,)),
            dma((nl,)), dma((nl,)),
            dma((n,)), dma((n,)),
        ],
        compiler_params=pltpu.CompilerParams(
            collective_id=0, has_side_effects=True, vmem_limit_bytes=32 * 1024 * 1024
        ),
    )(eps_lin, eps_loss, kerr_coef, region, core_mask, intensity, right_side.reshape(flat), start_field.reshape(flat))
    return out.reshape(right_side.shape)


def solution(mesh):
    placed = (
        P(None, None, None, "prop", "lat", None),
        P(None, None, None, "prop", "lat", None),
        P("prop", "lat", None),
        P("prop", "lat", None),
        P("prop", "lat", None),
        P(),
        P(),
        P(),
    )
    return jax.shard_map(
        functools.partial(per_device, mesh.shape["prop"], mesh.shape["lat"]),
        mesh=mesh,
        in_specs=placed,
        out_specs=P(None, None, None, "prop", "lat", None),
        check_vma=False,
    )
```

```python
import functools

import jax
import jax.numpy as jnp
from jax import lax
from jax.experimental import pallas as pl
from jax.experimental.pallas import tpu as pltpu
from jax.sharding import PartitionSpec as P

MESH = pl.DeviceIdType.MESH
wave_sq = 0.25
wave_shift = 0.02
loss_gain = 3.2
tiny = 1e-06


def cmul(a, b):
    return (a[0] * b[0] - a[1] * b[1], a[0] * b[1] + a[1] * b[0])


def cadd(a, b):
    return (a[0] + b[0], a[1] + b[1])


def cinv(a):
    scale = 1.0 / (a[0] * a[0] + a[1] * a[1])
    return (a[0] * scale, -a[1] * scale)


def kernel(
    dims, lin_ref, loss_ref, kerr_ref, region_hbm, mask_hbm, inten_hbm, rhs_hbm, start_hbm, pre_hbm, size_ref,
    region_ref, mask_ref, inten_ref, rhs_ref, start_ref, out_ref, load_sem, known,
    field, resid, local, pre, cell, corner, corner_all, link, tips_out, tips_in, ends_out, ends_in, part,
    lat_parts, prop_parts,
    halo_send, halo_recv, corner_send, corner_recv, tips_send, tips_recv, ends_send, ends_recv,
    pre_send, pre_recv, lat_send, lat_recv, prop_send, prop_recv,
):
    n, nl, S, Z, X, NY, u, m, rows, together = dims
    NREG = lin_ref.shape[0]
    lat = lax.axis_index("lat")
    prop = lax.axis_index("prop")
    has_up, has_down = prop + 1 < n, prop > 0
    has_right, has_left = lat + 1 < nl, lat > 0
    ZX = Z * X

    def at_prop(q):
        return {"lat": lat, "prop": q}

    def at(l, q):
        return {"lat": l, "prop": q}

    def others(count, me, act):
        def body(j, carry):
            act(lax.rem(me + j, count))
            return carry

        lax.fori_loop(1, count, body, 0, unroll=True)

    pairs = (
        (start_hbm, start_ref), (region_hbm, region_ref), (mask_hbm, mask_ref), (inten_hbm, inten_ref), (rhs_hbm, rhs_ref)
    )
    loads = [pltpu.make_async_copy(src, dst, load_sem.at[i]) for i, (src, dst) in enumerate(pairs)]
    for load in loads:
        load.start()
    barrier = pltpu.get_barrier_semaphore()

    def greet(l, q):
        pl.semaphore_signal(barrier, inc=1, device_id=at(l, q), device_id_type=MESH)

    diag_up = jnp.logical_and(has_left, has_up)
    diag_down = jnp.logical_and(has_right, has_down)
    bits = [("lat", 1 << i) for i in range(nl.bit_length() - 1)] + [("prop", 1 << i) for i in range(n.bit_length() - 1)]

    def facing(axis, bit):
        return at(lat ^ bit, prop) if axis == "lat" else at(lat, prop ^ bit)

    for axis, bit in bits:
        pl.semaphore_signal(barrier, inc=1, device_id=facing(axis, bit), device_id_type=MESH)
    pl.when(has_right)(lambda: greet(lat + 1, prop))
    pl.when(has_left)(lambda: greet(lat - 1, prop))
    pl.when(has_up)(lambda: greet(lat, prop + 1))
    pl.when(has_down)(lambda: greet(lat, prop - 1))
    pl.when(diag_up)(lambda: greet(lat - 1, prop + 1))
    pl.when(diag_down)(lambda: greet(lat + 1, prop - 1))

    zero_plane = jnp.zeros((X, S, NY), jnp.float32)
    zero_line = jnp.zeros((S, NY), jnp.float32)
    loads[0].wait()
    for c in range(2):
        for k in range(3):
            for z in range(Z):
                for x in range(X):
                    base = (c * 3 + k) * S * ZX + z * X + x
                    field[c, k, z + 1, x + 1] = start_ref[pl.ds(base, S, stride=ZX), :]

    def clear(cond, buf, planes, xs):
        @pl.when(cond)
        def _():
            for c in range(2):
                for k in range(3):
                    for z in planes:
                        for x in xs:
                            buf[c, k, z, x] = zero_line

    no_up, no_down = jnp.logical_not(has_up), jnp.logical_not(has_down)
    no_right, no_left = jnp.logical_not(has_right), jnp.logical_not(has_left)
    inner_z, inner_x = range(1, Z + 1), range(1, X + 1)
    for buf, wide in ((field, inner_z), (pre, range(Z + 2))):
        clear(no_left, buf, wide, (0,))
        clear(no_right, buf, wide, (X + 1,))
    clear(no_down, field, (0,), inner_x)
    clear(no_up, field, (Z + 1,), inner_x)
    clear(jnp.logical_or(no_down, no_right), field, (0,), (X + 1,))
    clear(jnp.logical_or(no_up, no_left), field, (Z + 1,), (0,))

    for load in loads[1:4]:
        load.wait()
    region = region_ref[...]
    lin = jnp.zeros((Z, X, NY), jnp.float32)
    loss = lin
    kerr = lin
    for r in range(NREG):
        hit = region == r
        lin = jnp.where(hit, lin_ref[r], lin)
        loss = jnp.where(hit, loss_ref[r], loss)
        kerr = jnp.where(hit, kerr_ref[r], kerr)
    perm_real = lin + mask_ref[...].astype(jnp.float32) * kerr * inten_ref[...]
    diag_real = 2.0 - wave_shift * perm_real
    diag_imag = loss_gain / (Z * n) * loss
    gains = []
    for z in range(Z):
        d = (diag_real[z], diag_imag[z])
        if z:
            d = (d[0] - gains[-1][0], d[1] - gains[-1][1])
        gains.append(cinv(d))
    front = [gains[0]]
    for z in range(1, Z):
        front.append(cmul(gains[z], front[-1]))
    from_below = [front[-1]]
    from_above = [gains[-1]]
    for z in range(Z - 2, -1, -1):
        from_below.insert(0, cadd(front[z], cmul(gains[z], from_below[0])))
        from_above.insert(0, cmul(gains[z], from_above[0]))
    for z in range(Z):
        kinds = (wave_sq * perm_real[z], wave_sq * loss[z], *gains[z], *from_below[z], *from_above[z])
        for i, value in enumerate(kinds):
            for x in range(X):
                cell[i, z, x] = value[x : x + 1, :]
    triple = (*from_below[0], *from_below[-1], *from_above[-1])
    for x in range(X):
        for i, value in enumerate(triple):
            corner[x, i : i + 1, :] = value[x : x + 1, :]
        corner[x, 6:8, :] = jnp.zeros((2, NY), jnp.float32)

    count = len(bits)
    for cond in (has_right, has_left, has_up, has_down, diag_up, diag_down):
        count = count + cond.astype(jnp.int32)
    pl.semaphore_wait(barrier, count)

    def remote(src, dst, send, recv, device):
        return pltpu.make_async_remote_copy(
            src_ref=src, dst_ref=dst, send_sem=send, recv_sem=recv, device_id=device, device_id_type=MESH
        )

    iz, ix = pl.ds(1, Z), pl.ds(1, X)
    halo = [
        (has_up, field.at[:, :, Z, ix], field.at[:, :, 0, ix], at(lat, prop + 1), has_down),
        (has_down, field.at[:, 0:2, 1, ix], field.at[:, 0:2, Z + 1, ix], at(lat, prop - 1), has_up),
        (diag_up, field.at[:, 2, Z, 1], field.at[:, 2, 0, X + 1], at(lat - 1, prop + 1), diag_down),
        (diag_down, field.at[:, 0, 1, X], field.at[:, 0, Z + 1, 0], at(lat + 1, prop - 1), diag_up),
        (has_right, field.at[:, :, iz, X], field.at[:, :, iz, 0], at(lat + 1, prop), has_left),
        (has_left, field.at[:, 1:3, iz, 1], field.at[:, 1:3, iz, X + 1], at(lat - 1, prop), has_right),
    ]
    halos = [
        (remote(src, dst, halo_send.at[i], halo_recv.at[i], device), out, into)
        for i, (out, src, dst, device, into) in enumerate(halo)
    ]
    for copy, out, _ in halos:
        pl.when(out)(copy.start)

    def corner_copy(q):
        return remote(corner.at[q // m], corner_all.at[prop], corner_send.at[q], corner_recv.at[prop], at_prop(q))

    lane = lax.broadcasted_iota(jnp.int32, (X, S, NY), 2)
    at_first, at_last = lane == 0, lane == NY - 1

    def after(v):
        return jnp.where(at_last, 0.0, pltpu.roll(v, NY - 1, 2))

    def before(v):
        return jnp.where(at_first, 0.0, pltpu.roll(v, 1, 2))

    def curl(buf, c, z):
        def get(k, dz, dx):
            return buf[c, k, z + 1 + dz, 1 + dx : 1 + dx + X]

        ux, uy, uz = get(0, 0, 0), get(1, 0, 0), get(2, 0, 0)
        ux_up, uy_up = get(0, 1, 0), get(1, 1, 0)
        uz_down = get(2, -1, 0)
        uy_right, uz_right = get(1, 0, 1), get(2, 0, 1)
        ux_left = get(0, 0, -1)
        t = uy_right - uy
        out_x = (
            t + 4.0 * ux - after(ux) - before(ux + t) - get(0, -1, 0) - ux_up
            + (uz_right - uz) - (get(2, -1, 1) - uz_down)
        )
        ab = (uz - uz_down) + (ux - ux_left)
        out_y = 4.0 * uy - get(1, -1, 0) - uy_up - get(1, 0, -1) - uy_right + after(ab) - ab
        e = uy_up - uy
        out_z = (
            e + 4.0 * uz - after(uz) - before(uz + e) - get(2, 0, -1) - uz_right
            + (ux_up - ux) - (get(0, 1, -1) - ux_left)
        )
        return (out_x, out_y, out_z), (ux, uy, uz)

    def operate(buf, z):
        pr, pi = cell[0, z], cell[1, z]
        curl_re, re = curl(buf, 0, z)
        curl_im, im = curl(buf, 1, z)
        out_re = [curl_re[k] - (pr * re[k] - pi * im[k]) for k in range(3)]
        out_im = [curl_im[k] - (pr * im[k] + pi * re[k]) for k in range(3)]
        return out_re, out_im

    def residual(z):
        for c, parts in enumerate(operate(field, z)):
            for k in range(3):
                for x in range(X):
                    base = (c * 3 + k) * S * ZX + z * X + x
                    resid[c, k, z, x] = rhs_ref[pl.ds(base, S, stride=ZX), :] - parts[k][x]

    def tell(i):
        if i < len(bits):
            pl.semaphore_signal(known.at[i], inc=1, device_id=facing(*bits[i]), device_id_type=MESH)

    def hear(i):
        if i < len(bits):
            pl.semaphore_wait(known.at[i], 1)
            tell(i + 1)

    tell(1)
    loads[4].wait()
    for i in (4, 5):
        pl.when(halos[i][2])(halos[i][0].wait_recv)
    heard = 1
    for z in range(1, Z - 1):
        hear(heard)
        heard += 1
        residual(z)
    hear(heard)
    for i in (0, 2):
        pl.when(halos[i][2])(halos[i][0].wait_recv)
    residual(0)
    for i in range(heard + 1, len(bits)):
        hear(i)
    others(n, prop, lambda q: corner_copy(q).start())
    corner_all[prop] = corner[prop // m]
    for i in (1, 3):
        pl.when(halos[i][2])(halos[i][0].wait_recv)
    if Z > 1:
        residual(Z - 1)

    def coef(i, z):
        return (cell[i, z], cell[i + 1, z])

    def slot(base, b, c, k, a):
        return base + ((b * 2 + c) * 3 + k) * u + a

    for k in range(3):
        held = None
        for z in range(Z):
            r = (resid[0, k, z], resid[1, k, z])
            if held is not None:
                r = cadd(r, held)
            held = cmul(coef(2, z), r)
            if z < Z - 1:
                local[0, k, z] = held[0]
                local[1, k, z] = held[1]
        local[0, k, Z - 1], local[1, k, Z - 1] = held
        last = held
        for z in range(Z - 2, -1, -1):
            held = cadd((local[0, k, z], local[1, k, z]), cmul(coef(2, z), held))
            local[0, k, z], local[1, k, z] = held
        for b, ends in enumerate((held, last)):
            for c in range(2):
                for x in range(X):
                    for a in range(u):
                        tips_out[pl.ds(slot(x * m * rows, b, c, k, a), m, stride=rows), :] = ends[c][x, a * m : (a + 1) * m]

    def block(q):
        return pl.ds(pl.multiple_of(q * rows, 8), rows)

    def tips_copy(q):
        return remote(tips_out.at[block(q)], tips_in.at[block(prop)], tips_send.at[q], tips_recv.at[prop], at_prop(q))

    others(n, prop, lambda q: tips_copy(q).start())
    tips_in[block(prop), :] = tips_out[block(prop), :]

    def corner_from(q):
        return remote(corner.at[q // m], corner_all.at[q], corner_send.at[q], corner_recv.at[q], at_prop(q))

    others(n, prop, lambda q: corner_from(q).wait_recv())
    beta = (jnp.zeros((1, NY), jnp.float32),) * 2

    def link_step(k, beta):
        first, cross, last = [(corner_all[k, 2 * i : 2 * i + 1, :], corner_all[k, 2 * i + 1 : 2 * i + 2, :]) for i in range(3)]
        fb = cmul(first, beta)
        gamma = cinv((1.0 - fb[0], -fb[1]))
        carry = cmul(cross, gamma)
        mix = cmul(carry, beta)
        for i, value in enumerate((*carry, *mix, *gamma, *cmul(gamma, first), *beta)):
            link[k, i] = value
        return cadd(last, cmul(cross, mix))

    for k in range(n):
        beta = link_step(k, beta)

    def tips_from(q):
        return remote(tips_out.at[block(q)], tips_in.at[block(q)], tips_send.at[q], tips_recv.at[q], at_prop(q))

    others(n, prop, lambda q: tips_from(q).wait_recv())
    span = 3 * u

    def linked(k, i):
        return (link[k, 2 * i], link[k, 2 * i + 1])

    def tip(k, b):
        return tuple(tips_in[k * rows + (b * 2 + c) * span : k * rows + (b * 2 + c + 1) * span, :] for c in range(2))

    def put(k, b, value):
        for c in range(2):
            ends_out[k * rows + (b * 2 + c) * span : k * rows + (b * 2 + c + 1) * span, :] = value[c]

    none = (jnp.zeros((span, NY), jnp.float32),) * 2
    alphas = [none]
    for k in range(n):
        alphas.append(
            cadd(cadd(tip(k, 1), cmul(linked(k, 1), tip(k, 0))), cmul(linked(k, 0), alphas[-1]))
        )
    first = none
    for k in range(n - 1, -1, -1):
        put(k, 1, first)
        source = cadd(cmul(linked(k, 2), tip(k, 0)), cmul(linked(k, 3), alphas[k]))
        first = cadd(source, cmul(linked(k, 0), first))
        put(k, 0, cadd(alphas[k], cmul(linked(k, 4), first)) if k else none)

    def ends_copy(q):
        return remote(ends_out.at[block(q)], ends_in.at[block(prop)], ends_send.at[q], ends_recv.at[prop], at_prop(q))

    def ends_from(q):
        return remote(ends_out.at[block(q)], ends_in.at[block(q)], ends_send.at[q], ends_recv.at[q], at_prop(q))

    others(n, prop, lambda q: ends_copy(q).start())
    ends_in[block(prop), :] = ends_out[block(prop), :]
    others(n, prop, lambda q: ends_from(q).wait_recv())

    for k in range(3):
        sides = []
        for b in range(2):
            for c in range(2):
                for x in range(X):
                    for a in range(u):
                        pre[c, k, b * (Z + 1), 1 + x, a * m : (a + 1) * m, :] = ends_in[
                            pl.ds(slot(x * m * rows, b, c, k, a), m, stride=rows), :
                        ]
            sides.append(tuple(pre[c, k, b * (Z + 1), 1 : 1 + X] for c in range(2)))
        for z in range(Z):
            value = cadd((local[0, k, z], local[1, k, z]), cadd(cmul(coef(4, z), sides[0]), cmul(coef(6, z), sides[1])))
            for c in range(2):
                pre[c, k, z + 1, 1 : 1 + X] = value[c]
    side = [
        (has_right, pre.at[:, :, pl.ds(1, Z + 1), X], pre.at[:, :, pl.ds(1, Z + 1), 0], at(lat + 1, prop), has_left),
        (has_left, pre.at[:, 1:3, pl.ds(0, Z + 1), 1], pre.at[:, 1:3, pl.ds(0, Z + 1), X + 1], at(lat - 1, prop), has_right),
    ]
    sides = [
        (remote(src, dst, pre_send.at[i], pre_recv.at[i], device), out, into)
        for i, (out, src, dst, device, into) in enumerate(side)
    ]
    for copy, out, _ in sides:
        pl.when(out)(copy.start)
    for c in range(2):
        for k in range(3):
            for z in range(Z):
                for x in range(X):
                    base = (c * 3 + k) * S * ZX + z * X + x
                    out_ref[pl.ds(base, S, stride=ZX), :] = pre[c, k, z + 1, x + 1]
    write = pltpu.make_async_copy(out_ref, pre_hbm, load_sem.at[0])
    write.start()
    for copy, _, into in sides:
        pl.when(into)(copy.wait_recv)

    cross_sum = zero_plane
    self_sum = zero_plane
    for z in range(Z):
        for c, parts in enumerate(operate(pre, z)):
            for k in range(3):
                cross_sum = cross_sum + resid[c, k, z] * parts[k]
                self_sum = self_sum + parts[k] * parts[k]
    column = lax.broadcasted_iota(jnp.int32, (S, NY), 0)
    place = lax.broadcasted_iota(jnp.int32, (S, NY), 1)
    on_cross, on_self = place == column, place == column + S
    totals = [jnp.sum(jnp.sum(v, axis=0), axis=1, keepdims=True) for v in (cross_sum, self_sum)]
    packed = jnp.where(on_cross, totals[0], jnp.where(on_self, totals[1], 0.0))
    row = jnp.sum(packed, axis=0, keepdims=True)

    def reduced(row, count, me, parts, i, send, recv, device):
        part[i] = row
        parts[me] = row

        def copy(q, own):
            return remote(part.at[i], parts.at[own], send.at[q], recv.at[own], device(q))

        others(count, me, lambda q: copy(q, me).start())
        others(count, me, lambda q: copy(q, q).wait_recv())
        others(count, me, lambda q: copy(q, q).wait_send())
        total = parts[0]
        for j in range(1, count):
            total = total + parts[j]
        return total

    if together:
        row = reduced(row, nl * n, lat * n + prop, prop_parts, 1, prop_send, prop_recv, lambda j: at(j // n, j % n))
    else:
        row = reduced(row, nl, lat, lat_parts, 0, lat_send, lat_recv, lambda l: at(l, prop))
        row = reduced(row, n, prop, prop_parts, 1, prop_send, prop_recv, at_prop)
    wide = jnp.broadcast_to(row, (S, NY))
    cross_total = jnp.sum(jnp.where(on_cross, wide, 0.0), axis=1, keepdims=True)
    self_total = jnp.sum(jnp.where(on_self, wide, 0.0), axis=1, keepdims=True)
    size_ref[...] = jnp.broadcast_to(cross_total / (self_total + tiny), (S, NY))
    write.wait()
    for copy, out, _ in halos + sides:
        pl.when(out)(copy.wait_send)
    others(n, prop, lambda q: corner_from(q).wait_send())
    others(n, prop, lambda q: tips_from(q).wait_send())
    others(n, prop, lambda q: ends_from(q).wait_send())


def per_device(n, nl, right_side, start_field, region, core_mask, intensity, eps_lin, eps_loss, kerr_coef):
    S, Z, X, NY = right_side.shape[2:]
    m = n // X
    u = S // m
    rows = -(-12 * u // 8) * 8
    together = n * nl <= 64
    team = n * nl if together else n
    dims = (n, nl, S, Z, X, NY, u, m, rows, together)
    flat = (6 * S * Z * X, NY)
    f32 = jnp.float32
    vmem = pl.BlockSpec(memory_space=pltpu.VMEM)
    smem = pl.BlockSpec(memory_space=pltpu.SMEM)
    dma = pltpu.SemaphoreType.DMA
    pre, size = pl.pallas_call(
        functools.partial(kernel, dims),
        out_shape=(jax.ShapeDtypeStruct(flat, f32), jax.ShapeDtypeStruct((S, NY), f32)),
        in_specs=[smem] * 3 + [pl.BlockSpec(memory_space=pltpu.HBM)] * 5,
        out_specs=(pl.BlockSpec(memory_space=pltpu.HBM), vmem),
        scratch_shapes=[
            pltpu.VMEM(region.shape, region.dtype),
            pltpu.VMEM(region.shape, core_mask.dtype),
            pltpu.VMEM(region.shape, f32),
            pltpu.VMEM(flat, f32),
            pltpu.VMEM(flat, f32),
            pltpu.VMEM(flat, f32),
            dma((5,)),
            pltpu.SemaphoreType.REGULAR((n.bit_length() + nl.bit_length(),)),
            pltpu.VMEM((2, 3, Z + 2, X + 2, S, NY), f32),
            pltpu.VMEM((2, 3, Z, X, S, NY), f32),
            pltpu.VMEM((2, 3, Z, X, S, NY), f32),
            pltpu.VMEM((2, 3, Z + 2, X + 2, S, NY), f32),
            pltpu.VMEM((8, Z, X, 1, NY), f32),
            pltpu.VMEM((X, 8, NY), f32),
            pltpu.VMEM((n, 8, NY), f32),
            pltpu.VMEM((n, 10, 1, NY), f32),
            pltpu.VMEM((n * rows, NY), f32),
            pltpu.VMEM((n * rows, NY), f32),
            pltpu.VMEM((n * rows, NY), f32),
            pltpu.VMEM((n * rows, NY), f32),
            pltpu.VMEM((2, 1, NY), f32),
            pltpu.VMEM((nl, 1, NY), f32),
            pltpu.VMEM((team, 1, NY), f32),
            dma((6,)), dma((6,)),
            dma((n,)), dma((n,)),
            dma((n,)), dma((n,)),
            dma((n,)), dma((n,)),
            dma((2,)), dma((2,)),
            dma((nl,)), dma((nl,)),
            dma((team,)), dma((team,)),
        ],
        compiler_params=pltpu.CompilerParams(
            collective_id=0, has_side_effects=True, vmem_limit_bytes=60 * 1024 * 1024
        ),
    )(eps_lin, eps_loss, kerr_coef, region, core_mask, intensity, right_side.reshape(flat), start_field.reshape(flat))
    return start_field + size.reshape(1, 1, S, 1, 1, NY) * pre.reshape(right_side.shape)


def solution(mesh):
    placed = (
        P(None, None, None, "prop", "lat", None),
        P(None, None, None, "prop", "lat", None),
        P("prop", "lat", None),
        P("prop", "lat", None),
        P("prop", "lat", None),
        P(),
        P(),
        P(),
    )
    return jax.shard_map(
        functools.partial(per_device, mesh.shape["prop"], mesh.shape["lat"]),
        mesh=mesh,
        in_specs=placed,
        out_specs=P(None, None, None, "prop", "lat", None),
        check_vma=False,
    )
```

```python
import functools

import jax
import jax.numpy as jnp
from jax import lax
from jax.experimental import pallas as pl
from jax.experimental.pallas import tpu as pltpu
from jax.sharding import PartitionSpec as P

MESH = pl.DeviceIdType.MESH
wave_sq = 0.25
wave_shift = 0.02
loss_gain = 3.2
tiny = 1e-06


def cmul(a, b):
    return (a[0] * b[0] - a[1] * b[1], a[0] * b[1] + a[1] * b[0])


def cadd(a, b):
    return (a[0] + b[0], a[1] + b[1])


def cinv(a):
    scale = 1.0 / (a[0] * a[0] + a[1] * a[1])
    return (a[0] * scale, -a[1] * scale)


def kernel(
    dims, lin_ref, loss_ref, kerr_ref, region_hbm, mask_hbm, inten_hbm, rhs_hbm, start_hbm, out_ref, size_ref,
    region_ref, mask_ref, inten_ref, rhs_ref, start_ref, load_sem, known,
    field, resid, local, pre, cell, corner, corner_all, link, tips_out, tips_in, ends_out, ends_in, part,
    lat_parts, prop_parts,
    halo_send, halo_recv, corner_send, corner_recv, tips_send, tips_recv, ends_send, ends_recv,
    pre_send, pre_recv, lat_send, lat_recv, prop_send, prop_recv,
):
    n, nl, S, Z, X, NY, ns, lo, u, m, rows, together = dims
    NREG = lin_ref.shape[0]
    lat = lax.axis_index("lat")
    prop = lax.axis_index("prop")
    has_up, has_down = prop + 1 < n, prop > 0
    has_right, has_left = lat + 1 < nl, lat > 0
    ZX = Z * X

    def at_prop(q):
        return {"lat": lat, "prop": q}

    def at(l, q):
        return {"lat": l, "prop": q}

    def others(count, me, act):
        for j in range(count - 1, 0, -1):
            act(me ^ j)

    pairs = (
        (start_hbm, start_ref), (region_hbm, region_ref), (mask_hbm, mask_ref), (inten_hbm, inten_ref), (rhs_hbm, rhs_ref)
    )
    loads = [pltpu.make_async_copy(src, dst, load_sem.at[i]) for i, (src, dst) in enumerate(pairs)]
    for load in loads:
        load.start()
    barrier = pltpu.get_barrier_semaphore()

    def greet(l, q):
        pl.semaphore_signal(barrier, inc=1, device_id=at(l, q), device_id_type=MESH)

    diag_up = jnp.logical_and(has_left, has_up)
    diag_down = jnp.logical_and(has_right, has_down)
    bits = [("lat", 1 << i) for i in range(nl.bit_length() - 1)] + [("prop", 1 << i) for i in range(n.bit_length() - 1)]

    def facing(axis, bit):
        return at(lat ^ bit, prop) if axis == "lat" else at(lat, prop ^ bit)

    for axis, bit in bits:
        pl.semaphore_signal(barrier, inc=1, device_id=facing(axis, bit), device_id_type=MESH)
    pl.when(has_right)(lambda: greet(lat + 1, prop))
    pl.when(has_left)(lambda: greet(lat - 1, prop))
    pl.when(has_up)(lambda: greet(lat, prop + 1))
    pl.when(has_down)(lambda: greet(lat, prop - 1))
    pl.when(diag_up)(lambda: greet(lat - 1, prop + 1))
    pl.when(diag_down)(lambda: greet(lat + 1, prop - 1))

    zero_plane = jnp.zeros((X, S, NY), jnp.float32)
    zero_line = jnp.zeros((S, NY), jnp.float32)
    loads[0].wait()
    for c in range(2):
        for k in range(3):
            for z in range(Z):
                for x in range(X):
                    base = (c * 3 + k) * S * ZX + z * X + x
                    field[c, k, z + 1, x + 1] = start_ref[pl.ds(base, S, stride=ZX), :]

    def clear(cond, buf, planes, xs):
        @pl.when(cond)
        def _():
            for c in range(2):
                for k in range(3):
                    for z in planes:
                        for x in xs:
                            buf[c, k, z, x] = zero_line

    no_up, no_down = jnp.logical_not(has_up), jnp.logical_not(has_down)
    no_right, no_left = jnp.logical_not(has_right), jnp.logical_not(has_left)
    inner_z, inner_x = range(1, Z + 1), range(1, X + 1)
    for buf, wide in ((field, inner_z), (pre, range(Z + 2))):
        clear(no_left, buf, wide, (0,))
        clear(no_right, buf, wide, (X + 1,))
    clear(no_down, field, (0,), inner_x)
    clear(no_up, field, (Z + 1,), inner_x)
    clear(jnp.logical_or(no_down, no_right), field, (0,), (X + 1,))
    clear(jnp.logical_or(no_up, no_left), field, (Z + 1,), (0,))

    count = len(bits)
    for cond in (has_right, has_left, has_up, has_down, diag_up, diag_down):
        count = count + cond.astype(jnp.int32)
    pl.semaphore_wait(barrier, count)

    def remote(src, dst, send, recv, device):
        return pltpu.make_async_remote_copy(
            src_ref=src, dst_ref=dst, send_sem=send, recv_sem=recv, device_id=device, device_id_type=MESH
        )

    iz, ix = pl.ds(1, Z), pl.ds(1, X)
    halo = [
        (has_up, field.at[:, :, Z, ix], field.at[:, :, 0, ix], at(lat, prop + 1), has_down),
        (has_down, field.at[:, 0:2, 1, ix], field.at[:, 0:2, Z + 1, ix], at(lat, prop - 1), has_up),
        (diag_up, field.at[:, 2, Z, 1], field.at[:, 2, 0, X + 1], at(lat - 1, prop + 1), diag_down),
        (diag_down, field.at[:, 0, 1, X], field.at[:, 0, Z + 1, 0], at(lat + 1, prop - 1), diag_up),
        (has_right, field.at[:, :, iz, X], field.at[:, :, iz, 0], at(lat + 1, prop), has_left),
        (has_left, field.at[:, 1:3, iz, 1], field.at[:, 1:3, iz, X + 1], at(lat - 1, prop), has_right),
    ]
    halos = [
        (remote(src, dst, halo_send.at[i], halo_recv.at[i], device), out, into)
        for i, (out, src, dst, device, into) in enumerate(halo)
    ]
    for copy, out, _ in halos:
        pl.when(out)(copy.start)

    mine = prop - lo
    couples = jnp.logical_and(mine >= 0, mine < ns)
    folded = lax.rem(mine + n, ns)

    def couplers(act):
        for j in range(ns - 1, 0, -1):
            act(folded ^ j)
        if ns < n:
            pl.when(jnp.logical_not(couples))(lambda: act(folded))

    def corner_copy(t):
        return remote(corner.at[t // m], corner_all.at[prop], corner_send.at[t], corner_recv.at[prop], at_prop(t + lo))

    def tell(i):
        if i < len(bits):
            pl.semaphore_signal(known.at[i], inc=1, device_id=facing(*bits[i]), device_id_type=MESH)

    def hear(i):
        if i < len(bits):
            pl.semaphore_wait(known.at[i], 1)
            tell(i + 1)

    tell(1)

    for load in loads[1:4]:
        load.wait()
    region = region_ref[...]
    lin = jnp.zeros((Z, X, NY), jnp.float32)
    loss = lin
    kerr = lin
    for r in range(NREG):
        hit = region == r
        lin = jnp.where(hit, lin_ref[r], lin)
        loss = jnp.where(hit, loss_ref[r], loss)
        kerr = jnp.where(hit, kerr_ref[r], kerr)
    perm_real = lin + mask_ref[...].astype(jnp.float32) * kerr * inten_ref[...]
    diag_real = 2.0 - wave_shift * perm_real
    diag_imag = loss_gain / (Z * n) * loss
    gains = []
    for z in range(Z):
        d = (diag_real[z], diag_imag[z])
        if z:
            d = (d[0] - gains[-1][0], d[1] - gains[-1][1])
        gains.append(cinv(d))
    front = [gains[0]]
    for z in range(1, Z):
        front.append(cmul(gains[z], front[-1]))
    from_below = [front[-1]]
    from_above = [gains[-1]]
    for z in range(Z - 2, -1, -1):
        from_below.insert(0, cadd(front[z], cmul(gains[z], from_below[0])))
        from_above.insert(0, cmul(gains[z], from_above[0]))
    for z in range(Z):
        kinds = (wave_sq * perm_real[z], wave_sq * loss[z], *gains[z], *from_below[z], *from_above[z])
        for i, value in enumerate(kinds):
            for x in range(X):
                cell[i, z, x] = value[x : x + 1, :]
    triple = (*from_below[0], *from_below[-1], *from_above[-1])
    for x in range(X):
        for i, value in enumerate(triple):
            corner[x, i : i + 1, :] = value[x : x + 1, :]
        corner[x, 6:8, :] = jnp.zeros((2, NY), jnp.float32)

    lane = lax.broadcasted_iota(jnp.int32, (X, S, NY), 2)
    at_first, at_last = lane == 0, lane == NY - 1

    def after(v):
        return jnp.where(at_last, 0.0, pltpu.roll(v, NY - 1, 2))

    def before(v):
        return jnp.where(at_first, 0.0, pltpu.roll(v, 1, 2))

    def curl(buf, c, z):
        def get(k, dz, dx):
            return buf[c, k, z + 1 + dz, 1 + dx : 1 + dx + X]

        ux, uy, uz = get(0, 0, 0), get(1, 0, 0), get(2, 0, 0)
        ux_up, uy_up = get(0, 1, 0), get(1, 1, 0)
        uz_down = get(2, -1, 0)
        uy_right, uz_right = get(1, 0, 1), get(2, 0, 1)
        ux_left = get(0, 0, -1)
        t = uy_right - uy
        out_x = (
            t + 4.0 * ux - after(ux) - before(ux + t) - get(0, -1, 0) - ux_up
            + (uz_right - uz) - (get(2, -1, 1) - uz_down)
        )
        ab = (uz - uz_down) + (ux - ux_left)
        out_y = 4.0 * uy - get(1, -1, 0) - uy_up - get(1, 0, -1) - uy_right + after(ab) - ab
        e = uy_up - uy
        out_z = (
            e + 4.0 * uz - after(uz) - before(uz + e) - get(2, 0, -1) - uz_right
            + (ux_up - ux) - (get(0, 1, -1) - ux_left)
        )
        return (out_x, out_y, out_z), (ux, uy, uz)

    def operate(buf, z):
        pr, pi = cell[0, z], cell[1, z]
        curl_re, re = curl(buf, 0, z)
        curl_im, im = curl(buf, 1, z)
        out_re = [curl_re[k] - (pr * re[k] - pi * im[k]) for k in range(3)]
        out_im = [curl_im[k] - (pr * im[k] + pi * re[k]) for k in range(3)]
        return out_re, out_im

    def residual(z):
        for c, parts in enumerate(operate(field, z)):
            for k in range(3):
                for x in range(X):
                    base = (c * 3 + k) * S * ZX + z * X + x
                    resid[c, k, z, x] = rhs_ref[pl.ds(base, S, stride=ZX), :] - parts[k][x]

    loads[4].wait()
    for i in (4, 5):
        pl.when(halos[i][2])(halos[i][0].wait_recv)
    heard = 1
    for z in range(1, Z - 1):
        hear(heard)
        heard += 1
        residual(z)
    hear(heard)
    for i in (0, 2):
        pl.when(halos[i][2])(halos[i][0].wait_recv)
    residual(0)
    for i in range(heard + 1, len(bits)):
        hear(i)
    couplers(lambda t: corner_copy(t).start())
    for i in (1, 3):
        pl.when(halos[i][2])(halos[i][0].wait_recv)
    if Z > 1:
        residual(Z - 1)

    def coef(i, z):
        return (cell[i, z], cell[i + 1, z])

    def slot(base, b, c, k, a):
        return base + ((b * 2 + c) * 3 + k) * u + a

    for k in range(3):
        held = None
        for z in range(Z):
            r = (resid[0, k, z], resid[1, k, z])
            if held is not None:
                r = cadd(r, held)
            held = cmul(coef(2, z), r)
            if z < Z - 1:
                local[0, k, z] = held[0]
                local[1, k, z] = held[1]
        local[0, k, Z - 1], local[1, k, Z - 1] = held
        last = held
        for z in range(Z - 2, -1, -1):
            held = cadd((local[0, k, z], local[1, k, z]), cmul(coef(2, z), held))
            local[0, k, z], local[1, k, z] = held
        for b, ends in enumerate((held, last)):
            for c in range(2):
                for x in range(X):
                    for a in range(u):
                        tips_out[pl.ds(slot(x * m * rows, b, c, k, a), m, stride=rows), :] = ends[c][x, a * m : (a + 1) * m]

    def block(q):
        return pl.ds(pl.multiple_of(q * rows, 8), rows)

    def tips_copy(t):
        return remote(tips_out.at[block(t)], tips_in.at[block(prop)], tips_send.at[t], tips_recv.at[prop], at_prop(t + lo))

    def tips_from(q):
        return remote(tips_out.at[block(0)], tips_in.at[block(q)], tips_send.at[0], tips_recv.at[q], at_prop(q))

    def corner_from(q):
        return remote(corner.at[0], corner_all.at[q], corner_send.at[0], corner_recv.at[q], at_prop(q))

    def ends_copy(q):
        return remote(ends_out.at[block(q)], ends_in.at[block(mine)], ends_send.at[q], ends_recv.at[mine], at_prop(q))

    def ends_from(t):
        return remote(ends_out.at[block(0)], ends_in.at[block(t)], ends_send.at[0], ends_recv.at[t], at_prop(t + lo))

    couplers(lambda t: tips_copy(t).start())

    def couple():
        tips_in[block(prop), :] = tips_out[block(mine), :]
        corner_all[prop] = corner[mine // m]
        others(n, prop, lambda q: corner_from(q).wait_recv())
        beta = (jnp.zeros((1, NY), jnp.float32),) * 2

        def link_step(k, beta):
            first, cross, last = [(corner_all[k, 2 * i : 2 * i + 1, :], corner_all[k, 2 * i + 1 : 2 * i + 2, :]) for i in range(3)]
            fb = cmul(first, beta)
            gamma = cinv((1.0 - fb[0], -fb[1]))
            carry = cmul(cross, gamma)
            mix = cmul(carry, beta)
            for i, value in enumerate((*carry, *mix, *gamma, *cmul(gamma, first), *beta)):
                link[k, i] = value
            return cadd(last, cmul(cross, mix))

        for k in range(n):
            beta = link_step(k, beta)

        others(n, prop, lambda q: tips_from(q).wait_recv())
        span = 3 * u

        def linked(k, i):
            return (link[k, 2 * i], link[k, 2 * i + 1])

        def tip(k, b):
            return tuple(tips_in[k * rows + (b * 2 + c) * span : k * rows + (b * 2 + c + 1) * span, :] for c in range(2))

        def put(k, b, value):
            for c in range(2):
                ends_out[k * rows + (b * 2 + c) * span : k * rows + (b * 2 + c + 1) * span, :] = value[c]

        none = (jnp.zeros((span, NY), jnp.float32),) * 2
        alphas = [none]
        for k in range(n):
            alphas.append(
                cadd(cadd(tip(k, 1), cmul(linked(k, 1), tip(k, 0))), cmul(linked(k, 0), alphas[-1]))
            )
        first = none
        for k in range(n - 1, -1, -1):
            put(k, 1, first)
            source = cadd(cmul(linked(k, 2), tip(k, 0)), cmul(linked(k, 3), alphas[k]))
            first = cadd(source, cmul(linked(k, 0), first))
            put(k, 0, cadd(alphas[k], cmul(linked(k, 4), first)) if k else none)

        others(n, prop, lambda q: ends_copy(q).start())
        ends_in[block(mine), :] = ends_out[block(prop), :]

    pl.when(couples)(couple)

    couplers(lambda t: ends_from(t).wait_recv())
    for k in range(3):
        sides = []
        for b in range(2):
            for c in range(2):
                for x in range(X):
                    for a in range(u):
                        pre[c, k, b * (Z + 1), 1 + x, a * m : (a + 1) * m, :] = ends_in[
                            pl.ds(slot(x * m * rows, b, c, k, a), m, stride=rows), :
                        ]
            sides.append(tuple(pre[c, k, b * (Z + 1), 1 : 1 + X] for c in range(2)))
        for z in range(Z):
            value = cadd((local[0, k, z], local[1, k, z]), cadd(cmul(coef(4, z), sides[0]), cmul(coef(6, z), sides[1])))
            for c in range(2):
                pre[c, k, z + 1, 1 : 1 + X] = value[c]
    side = [
        (has_right, pre.at[:, :, pl.ds(1, Z + 1), X], pre.at[:, :, pl.ds(1, Z + 1), 0], at(lat + 1, prop), has_left),
        (has_left, pre.at[:, 1:3, pl.ds(0, Z + 1), 1], pre.at[:, 1:3, pl.ds(0, Z + 1), X + 1], at(lat - 1, prop), has_right),
    ]
    sides = [
        (remote(src, dst, pre_send.at[i], pre_recv.at[i], device), out, into)
        for i, (out, src, dst, device, into) in enumerate(side)
    ]
    for copy, out, _ in sides:
        pl.when(out)(copy.start)
    for c in range(2):
        for k in range(3):
            for z in range(Z):
                for x in range(X):
                    base = (c * 3 + k) * S * ZX + z * X + x
                    out_ref[pl.ds(base, S, stride=ZX), :] = pre[c, k, z + 1, x + 1]
    for copy, _, into in sides:
        pl.when(into)(copy.wait_recv)

    cross_sum = zero_plane
    self_sum = zero_plane
    for z in range(Z):
        for c, parts in enumerate(operate(pre, z)):
            for k in range(3):
                cross_sum = cross_sum + resid[c, k, z] * parts[k]
                self_sum = self_sum + parts[k] * parts[k]
    column = lax.broadcasted_iota(jnp.int32, (S, NY), 0)
    place = lax.broadcasted_iota(jnp.int32, (S, NY), 1)
    on_cross, on_self = place == column, place == column + S
    totals = [jnp.sum(jnp.sum(v, axis=0), axis=1, keepdims=True) for v in (cross_sum, self_sum)]
    packed = jnp.where(on_cross, totals[0], jnp.where(on_self, totals[1], 0.0))
    row = jnp.sum(packed, axis=0, keepdims=True)

    def reduced(row, count, me, parts, i, send, recv, device):
        part[i] = row
        parts[me] = row

        def copy(q, own):
            return remote(part.at[i], parts.at[own], send.at[q], recv.at[own], device(q))

        others(count, me, lambda q: copy(q, me).start())
        others(count, me, lambda q: copy(q, q).wait_recv())
        others(count, me, lambda q: copy(q, q).wait_send())
        total = parts[0]
        for j in range(1, count):
            total = total + parts[j]
        return total

    if together:
        row = reduced(row, nl * n, lat * n + prop, prop_parts, 1, prop_send, prop_recv, lambda j: at(j // n, j % n))
    else:
        row = reduced(row, nl, lat, lat_parts, 0, lat_send, lat_recv, lambda l: at(l, prop))
        row = reduced(row, n, prop, prop_parts, 1, prop_send, prop_recv, at_prop)
    wide = jnp.broadcast_to(row, (S, NY))
    cross_total = jnp.sum(jnp.where(on_cross, wide, 0.0), axis=1, keepdims=True)
    self_total = jnp.sum(jnp.where(on_self, wide, 0.0), axis=1, keepdims=True)
    size_ref[...] = jnp.broadcast_to(cross_total / (self_total + tiny), (S, NY))
    for copy, out, _ in halos + sides:
        pl.when(out)(copy.wait_send)
    couplers(lambda t: corner_copy(t).wait_send())
    couplers(lambda t: tips_copy(t).wait_send())
    pl.when(couples)(lambda: others(n, prop, lambda q: ends_copy(q).wait_send()))


def per_device(n, nl, right_side, start_field, region, core_mask, intensity, eps_lin, eps_loss, kerr_coef):
    S, Z, X, NY = right_side.shape[2:]
    ns = n
    lo = (n - ns) // 2
    m = ns // X
    u = S // m
    rows = -(-12 * u // 8) * 8
    together = n * nl <= 64
    team = n * nl if together else n
    dims = (n, nl, S, Z, X, NY, ns, lo, u, m, rows, together)
    flat = (6 * S * Z * X, NY)
    f32 = jnp.float32
    vmem = pl.BlockSpec(memory_space=pltpu.VMEM)
    smem = pl.BlockSpec(memory_space=pltpu.SMEM)
    dma = pltpu.SemaphoreType.DMA
    pre, size = pl.pallas_call(
        functools.partial(kernel, dims),
        out_shape=(pltpu.VMEM(flat, f32), pltpu.VMEM((S, NY), f32)),
        in_specs=[smem] * 3 + [pl.BlockSpec(memory_space=pltpu.HBM)] * 5,
        out_specs=(vmem, vmem),
        scratch_shapes=[
            pltpu.VMEM(region.shape, region.dtype),
            pltpu.VMEM(region.shape, core_mask.dtype),
            pltpu.VMEM(region.shape, f32),
            pltpu.VMEM(flat, f32),
            pltpu.VMEM(flat, f32),
            dma((5,)),
            pltpu.SemaphoreType.REGULAR((n.bit_length() + nl.bit_length(),)),
            pltpu.VMEM((2, 3, Z + 2, X + 2, S, NY), f32),
            pltpu.VMEM((2, 3, Z, X, S, NY), f32),
            pltpu.VMEM((2, 3, Z, X, S, NY), f32),
            pltpu.VMEM((2, 3, Z + 2, X + 2, S, NY), f32),
            pltpu.VMEM((8, Z, X, 1, NY), f32),
            pltpu.VMEM((X, 8, NY), f32),
            pltpu.VMEM((n, 8, NY), f32),
            pltpu.VMEM((n, 10, 1, NY), f32),
            pltpu.VMEM((ns * rows, NY), f32),
            pltpu.VMEM((n * rows, NY), f32),
            pltpu.VMEM((n * rows, NY), f32),
            pltpu.VMEM((ns * rows, NY), f32),
            pltpu.VMEM((2, 1, NY), f32),
            pltpu.VMEM((nl, 1, NY), f32),
            pltpu.VMEM((team, 1, NY), f32),
            dma((6,)), dma((6,)),
            dma((n,)), dma((n,)),
            dma((n,)), dma((n,)),
            dma((n,)), dma((n,)),
            dma((2,)), dma((2,)),
            dma((nl,)), dma((nl,)),
            dma((team,)), dma((team,)),
        ],
        compiler_params=pltpu.CompilerParams(
            collective_id=0, has_side_effects=True, vmem_limit_bytes=60 * 1024 * 1024
        ),
    )(eps_lin, eps_loss, kerr_coef, region, core_mask, intensity, right_side.reshape(flat), start_field.reshape(flat))
    tiled = (6, S, Z * X, NY)
    new = start_field.reshape(tiled) + size.reshape(1, S, 1, NY) * pre.reshape(tiled)
    return new.reshape(right_side.shape)


def solution(mesh):
    placed = (
        P(None, None, None, "prop", "lat", None),
        P(None, None, None, "prop", "lat", None),
        P("prop", "lat", None),
        P("prop", "lat", None),
        P("prop", "lat", None),
        P(),
        P(),
        P(),
    )
    return jax.shard_map(
        functools.partial(per_device, mesh.shape["prop"], mesh.shape["lat"]),
        mesh=mesh,
        in_specs=placed,
        out_specs=P(None, None, None, "prop", "lat", None),
        check_vma=False,
    )
```

```python
import functools

import jax
import jax.numpy as jnp
from jax import lax
from jax.experimental import pallas as pl
from jax.experimental.pallas import tpu as pltpu
from jax.sharding import PartitionSpec as P

MESH = pl.DeviceIdType.MESH
wave_sq = 0.25
wave_shift = 0.02
loss_gain = 3.2
tiny = 1e-06


def cmul(a, b):
    return (a[0] * b[0] - a[1] * b[1], a[0] * b[1] + a[1] * b[0])


def cadd(a, b):
    return (a[0] + b[0], a[1] + b[1])


def cinv(a):
    scale = 1.0 / (a[0] * a[0] + a[1] * a[1])
    return (a[0] * scale, -a[1] * scale)


def kernel(
    dims, lin_ref, loss_ref, kerr_ref, region_hbm, mask_hbm, inten_hbm, rhs_hbm, start_hbm, out_ref,
    region_ref, mask_ref, inten_ref, rhs_ref, start_ref, load_sem, known,
    field, resid, local, pre, cell, corner, corner_all, link, tips_out, tips_in, ends_out, ends_in, part,
    lat_parts, prop_parts,
    halo_send, halo_recv, corner_send, corner_recv, tips_send, tips_recv, ends_send, ends_recv,
    pre_send, pre_recv, lat_send, lat_recv, prop_send, prop_recv,
):
    n, nl, S, Z, X, NY, ns, lo, u, m, rows, together = dims
    NREG = lin_ref.shape[0]
    lat = lax.axis_index("lat")
    prop = lax.axis_index("prop")
    has_up, has_down = prop + 1 < n, prop > 0
    has_right, has_left = lat + 1 < nl, lat > 0
    ZX = Z * X

    def at_prop(q):
        return {"lat": lat, "prop": q}

    def at(l, q):
        return {"lat": l, "prop": q}

    def others(count, me, act):
        for j in range(count - 1, 0, -1):
            act(me ^ j)

    pairs = (
        (start_hbm, start_ref), (region_hbm, region_ref), (mask_hbm, mask_ref), (inten_hbm, inten_ref), (rhs_hbm, rhs_ref)
    )
    loads = [pltpu.make_async_copy(src, dst, load_sem.at[i]) for i, (src, dst) in enumerate(pairs)]
    for load in loads:
        load.start()
    barrier = pltpu.get_barrier_semaphore()

    def greet(l, q):
        pl.semaphore_signal(barrier, inc=1, device_id=at(l, q), device_id_type=MESH)

    diag_up = jnp.logical_and(has_left, has_up)
    diag_down = jnp.logical_and(has_right, has_down)
    bits = [("lat", 1 << i) for i in range(nl.bit_length() - 1)] + [("prop", 1 << i) for i in range(n.bit_length() - 1)]

    def facing(axis, bit):
        return at(lat ^ bit, prop) if axis == "lat" else at(lat, prop ^ bit)

    for axis, bit in bits:
        pl.semaphore_signal(barrier, inc=1, device_id=facing(axis, bit), device_id_type=MESH)
    pl.when(has_right)(lambda: greet(lat + 1, prop))
    pl.when(has_left)(lambda: greet(lat - 1, prop))
    pl.when(has_up)(lambda: greet(lat, prop + 1))
    pl.when(has_down)(lambda: greet(lat, prop - 1))
    pl.when(diag_up)(lambda: greet(lat - 1, prop + 1))
    pl.when(diag_down)(lambda: greet(lat + 1, prop - 1))

    zero_plane = jnp.zeros((X, S, NY), jnp.float32)
    zero_line = jnp.zeros((S, NY), jnp.float32)
    loads[0].wait()
    for c in range(2):
        for k in range(3):
            for z in range(Z):
                for x in range(X):
                    base = (c * 3 + k) * S * ZX + z * X + x
                    field[c, k, z + 1, x + 1] = start_ref[pl.ds(base, S, stride=ZX), :]

    def clear(cond, buf, planes, xs):
        @pl.when(cond)
        def _():
            for c in range(2):
                for k in range(3):
                    for z in planes:
                        for x in xs:
                            buf[c, k, z, x] = zero_line

    no_up, no_down = jnp.logical_not(has_up), jnp.logical_not(has_down)
    no_right, no_left = jnp.logical_not(has_right), jnp.logical_not(has_left)
    inner_z, inner_x = range(1, Z + 1), range(1, X + 1)
    for buf, wide in ((field, inner_z), (pre, range(Z + 2))):
        clear(no_left, buf, wide, (0,))
        clear(no_right, buf, wide, (X + 1,))
    clear(no_down, field, (0,), inner_x)
    clear(no_up, field, (Z + 1,), inner_x)
    clear(jnp.logical_or(no_down, no_right), field, (0,), (X + 1,))
    clear(jnp.logical_or(no_up, no_left), field, (Z + 1,), (0,))

    count = len(bits)
    for cond in (has_right, has_left, has_up, has_down, diag_up, diag_down):
        count = count + cond.astype(jnp.int32)
    pl.semaphore_wait(barrier, count)

    def remote(src, dst, send, recv, device):
        return pltpu.make_async_remote_copy(
            src_ref=src, dst_ref=dst, send_sem=send, recv_sem=recv, device_id=device, device_id_type=MESH
        )

    def whole(ref, sem):
        pltpu.make_async_copy(ref, ref, sem).wait()

    iz, ix = pl.ds(1, Z), pl.ds(1, X)
    halo = [
        (has_up, field.at[:, :, Z, ix], field.at[:, :, 0, ix], at(lat, prop + 1), has_down),
        (has_down, field.at[:, 0:2, 1, ix], field.at[:, 0:2, Z + 1, ix], at(lat, prop - 1), has_up),
        (diag_up, field.at[:, 2, Z, 1], field.at[:, 2, 0, X + 1], at(lat - 1, prop + 1), diag_down),
        (diag_down, field.at[:, 0, 1, X], field.at[:, 0, Z + 1, 0], at(lat + 1, prop - 1), diag_up),
        (has_right, field.at[:, :, iz, X], field.at[:, :, iz, 0], at(lat + 1, prop), has_left),
        (has_left, field.at[:, 1:3, iz, 1], field.at[:, 1:3, iz, X + 1], at(lat - 1, prop), has_right),
    ]
    halos = [
        (remote(src, dst, halo_send.at[i], halo_recv.at[i], device), out, into)
        for i, (out, src, dst, device, into) in enumerate(halo)
    ]
    for copy, out, _ in halos:
        pl.when(out)(copy.start)

    mine = prop - lo
    couples = jnp.logical_and(mine >= 0, mine < ns)
    folded = lax.rem(mine + n, ns)

    def couplers(act):
        for j in range(ns - 1, 0, -1):
            act(folded ^ j)
        if ns < n:
            pl.when(jnp.logical_not(couples))(lambda: act(folded))

    def corner_copy(t):
        return remote(corner.at[t // m], corner_all.at[prop], corner_send.at[0], corner_recv.at[0], at_prop(t + lo))

    def tell(i):
        if i < len(bits):
            pl.semaphore_signal(known.at[i], inc=1, device_id=facing(*bits[i]), device_id_type=MESH)

    def hear(i):
        if i < len(bits):
            pl.semaphore_wait(known.at[i], 1)
            tell(i + 1)

    tell(1)

    for load in loads[1:4]:
        load.wait()
    region = region_ref[...]
    lin = jnp.zeros((Z, X, NY), jnp.float32)
    loss = lin
    kerr = lin
    for r in range(NREG):
        hit = region == r
        lin = jnp.where(hit, lin_ref[r], lin)
        loss = jnp.where(hit, loss_ref[r], loss)
        kerr = jnp.where(hit, kerr_ref[r], kerr)
    perm_real = lin + mask_ref[...].astype(jnp.float32) * kerr * inten_ref[...]
    diag_real = 2.0 - wave_shift * perm_real
    diag_imag = loss_gain / (Z * n) * loss
    gains = []
    for z in range(Z):
        d = (diag_real[z], diag_imag[z])
        if z:
            d = (d[0] - gains[-1][0], d[1] - gains[-1][1])
        gains.append(cinv(d))
    front = [gains[0]]
    for z in range(1, Z):
        front.append(cmul(gains[z], front[-1]))
    from_below = [front[-1]]
    from_above = [gains[-1]]
    for z in range(Z - 2, -1, -1):
        from_below.insert(0, cadd(front[z], cmul(gains[z], from_below[0])))
        from_above.insert(0, cmul(gains[z], from_above[0]))
    for z in range(Z):
        kinds = (wave_sq * perm_real[z], wave_sq * loss[z], *gains[z], *from_below[z], *from_above[z])
        for i, value in enumerate(kinds):
            for x in range(X):
                cell[i, z, x] = value[x : x + 1, :]
    triple = (*from_below[0], *from_below[-1], *from_above[-1])
    for x in range(X):
        for i, value in enumerate(triple):
            corner[x, i : i + 1, :] = value[x : x + 1, :]
        corner[x, 6:8, :] = jnp.zeros((2, NY), jnp.float32)

    lane = lax.broadcasted_iota(jnp.int32, (X, S, NY), 2)
    at_first, at_last = lane == 0, lane == NY - 1

    def after(v):
        return jnp.where(at_last, 0.0, pltpu.roll(v, NY - 1, 2))

    def before(v):
        return jnp.where(at_first, 0.0, pltpu.roll(v, 1, 2))

    def curl(buf, c, z):
        def get(k, dz, dx):
            return buf[c, k, z + 1 + dz, 1 + dx : 1 + dx + X]

        ux, uy, uz = get(0, 0, 0), get(1, 0, 0), get(2, 0, 0)
        ux_up, uy_up = get(0, 1, 0), get(1, 1, 0)
        uz_down = get(2, -1, 0)
        uy_right, uz_right = get(1, 0, 1), get(2, 0, 1)
        ux_left = get(0, 0, -1)
        t = uy_right - uy
        out_x = (
            t + 4.0 * ux - after(ux) - before(ux + t) - get(0, -1, 0) - ux_up
            + (uz_right - uz) - (get(2, -1, 1) - uz_down)
        )
        ab = (uz - uz_down) + (ux - ux_left)
        out_y = 4.0 * uy - get(1, -1, 0) - uy_up - get(1, 0, -1) - uy_right + after(ab) - ab
        e = uy_up - uy
        out_z = (
            e + 4.0 * uz - after(uz) - before(uz + e) - get(2, 0, -1) - uz_right
            + (ux_up - ux) - (get(0, 1, -1) - ux_left)
        )
        return (out_x, out_y, out_z), (ux, uy, uz)

    def operate(buf, z):
        pr, pi = cell[0, z], cell[1, z]
        curl_re, re = curl(buf, 0, z)
        curl_im, im = curl(buf, 1, z)
        out_re = [curl_re[k] - (pr * re[k] - pi * im[k]) for k in range(3)]
        out_im = [curl_im[k] - (pr * im[k] + pi * re[k]) for k in range(3)]
        return out_re, out_im

    def residual(z):
        for c, parts in enumerate(operate(field, z)):
            for k in range(3):
                for x in range(X):
                    base = (c * 3 + k) * S * ZX + z * X + x
                    resid[c, k, z, x] = rhs_ref[pl.ds(base, S, stride=ZX), :] - parts[k][x]

    loads[4].wait()
    for i in (4, 5):
        pl.when(halos[i][2])(halos[i][0].wait_recv)
    heard = 1
    for z in range(1, Z - 1):
        hear(heard)
        heard += 1
        residual(z)
    hear(heard)
    for i in (0, 2):
        pl.when(halos[i][2])(halos[i][0].wait_recv)
    residual(0)
    for i in range(heard + 1, len(bits)):
        hear(i)
    couplers(lambda t: corner_copy(t).start())
    for i in (1, 3):
        pl.when(halos[i][2])(halos[i][0].wait_recv)
    if Z > 1:
        residual(Z - 1)

    def coef(i, z):
        return (cell[i, z], cell[i + 1, z])

    def slot(base, b, c, k, a):
        return base + ((b * 2 + c) * 3 + k) * u + a

    for k in range(3):
        held = None
        for z in range(Z):
            r = (resid[0, k, z], resid[1, k, z])
            if held is not None:
                r = cadd(r, held)
            held = cmul(coef(2, z), r)
            if z < Z - 1:
                local[0, k, z] = held[0]
                local[1, k, z] = held[1]
        local[0, k, Z - 1], local[1, k, Z - 1] = held
        last = held
        for z in range(Z - 2, -1, -1):
            held = cadd((local[0, k, z], local[1, k, z]), cmul(coef(2, z), held))
            local[0, k, z], local[1, k, z] = held
        for b, ends in enumerate((held, last)):
            for c in range(2):
                for x in range(X):
                    for a in range(u):
                        tips_out[pl.ds(slot(x * m * rows, b, c, k, a), m, stride=rows), :] = ends[c][x, a * m : (a + 1) * m]

    def block(q):
        return pl.ds(pl.multiple_of(q * rows, 8), rows)

    def tips_copy(t):
        return remote(tips_out.at[block(t)], tips_in.at[block(prop)], tips_send.at[0], tips_recv.at[0], at_prop(t + lo))

    def tips_from(q):
        return remote(tips_out.at[block(0)], tips_in.at[block(q)], tips_send.at[0], tips_recv.at[q], at_prop(q))

    def corner_from(q):
        return remote(corner.at[0], corner_all.at[q], corner_send.at[0], corner_recv.at[q], at_prop(q))

    def ends_copy(q):
        return remote(ends_out.at[block(q)], ends_in.at[block(mine)], ends_send.at[0], ends_recv.at[0], at_prop(q))

    def ends_from(t):
        return remote(ends_out.at[block(0)], ends_in.at[block(t)], ends_send.at[0], ends_recv.at[t], at_prop(t + lo))

    couplers(lambda t: tips_copy(t).start())

    def couple():
        tips_in[block(prop), :] = tips_out[block(mine), :]
        corner_all[prop] = corner[mine // m]
        whole(corner_all.at[pl.ds(0, n - 1)], corner_recv.at[0])
        beta = (jnp.zeros((1, NY), jnp.float32),) * 2

        def link_step(k, beta):
            first, cross, last = [(corner_all[k, 2 * i : 2 * i + 1, :], corner_all[k, 2 * i + 1 : 2 * i + 2, :]) for i in range(3)]
            fb = cmul(first, beta)
            gamma = cinv((1.0 - fb[0], -fb[1]))
            carry = cmul(cross, gamma)
            mix = cmul(carry, beta)
            for i, value in enumerate((*carry, *mix, *gamma, *cmul(gamma, first), *beta)):
                link[k, i] = value
            return cadd(last, cmul(cross, mix))

        for k in range(n):
            beta = link_step(k, beta)

        whole(tips_in.at[pl.ds(0, (n - 1) * rows)], tips_recv.at[0])
        span = 3 * u

        def linked(k, i):
            return (link[k, 2 * i], link[k, 2 * i + 1])

        def tip(k, b):
            return tuple(tips_in[k * rows + (b * 2 + c) * span : k * rows + (b * 2 + c + 1) * span, :] for c in range(2))

        def put(k, b, value):
            for c in range(2):
                ends_out[k * rows + (b * 2 + c) * span : k * rows + (b * 2 + c + 1) * span, :] = value[c]

        none = (jnp.zeros((span, NY), jnp.float32),) * 2
        alphas = [none]
        for k in range(n):
            alphas.append(
                cadd(cadd(tip(k, 1), cmul(linked(k, 1), tip(k, 0))), cmul(linked(k, 0), alphas[-1]))
            )
        first = none
        for k in range(n - 1, -1, -1):
            put(k, 1, first)
            source = cadd(cmul(linked(k, 2), tip(k, 0)), cmul(linked(k, 3), alphas[k]))
            first = cadd(source, cmul(linked(k, 0), first))
            put(k, 0, cadd(alphas[k], cmul(linked(k, 4), first)) if k else none)

        others(n, prop, lambda q: ends_copy(q).start())
        ends_in[block(mine), :] = ends_out[block(prop), :]

    pl.when(couples)(couple)

    whole(ends_in.at[pl.ds(0, (n - 1) * rows)], ends_recv.at[0])
    for k in range(3):
        sides = []
        for b in range(2):
            for c in range(2):
                for x in range(X):
                    for a in range(u):
                        pre[c, k, b * (Z + 1), 1 + x, a * m : (a + 1) * m, :] = ends_in[
                            pl.ds(slot(x * m * rows, b, c, k, a), m, stride=rows), :
                        ]
            sides.append(tuple(pre[c, k, b * (Z + 1), 1 : 1 + X] for c in range(2)))
        for z in range(Z):
            value = cadd((local[0, k, z], local[1, k, z]), cadd(cmul(coef(4, z), sides[0]), cmul(coef(6, z), sides[1])))
            for c in range(2):
                pre[c, k, z + 1, 1 : 1 + X] = value[c]
    side = [
        (has_right, pre.at[:, :, pl.ds(1, Z + 1), X], pre.at[:, :, pl.ds(1, Z + 1), 0], at(lat + 1, prop), has_left),
        (has_left, pre.at[:, 1:3, pl.ds(0, Z + 1), 1], pre.at[:, 1:3, pl.ds(0, Z + 1), X + 1], at(lat - 1, prop), has_right),
    ]
    sides = [
        (remote(src, dst, pre_send.at[i], pre_recv.at[i], device), out, into)
        for i, (out, src, dst, device, into) in enumerate(side)
    ]
    for copy, out, _ in sides:
        pl.when(out)(copy.start)
    for copy, _, into in sides:
        pl.when(into)(copy.wait_recv)

    cross_sum = zero_plane
    self_sum = zero_plane
    for z in range(Z):
        for c, parts in enumerate(operate(pre, z)):
            for k in range(3):
                cross_sum = cross_sum + resid[c, k, z] * parts[k]
                self_sum = self_sum + parts[k] * parts[k]
    column = lax.broadcasted_iota(jnp.int32, (S, NY), 0)
    place = lax.broadcasted_iota(jnp.int32, (S, NY), 1)
    on_cross, on_self = place == column, place == column + S
    totals = [jnp.sum(jnp.sum(v, axis=0), axis=1, keepdims=True) for v in (cross_sum, self_sum)]
    packed = jnp.where(on_cross, totals[0], jnp.where(on_self, totals[1], 0.0))
    row = jnp.sum(packed, axis=0, keepdims=True)

    def reduced(row, count, me, parts, i, send, recv, device):
        part[i] = row
        parts[me] = row

        def copy(q, own):
            return remote(part.at[i], parts.at[own], send.at[0], recv.at[0], device(q))

        others(count, me, lambda q: copy(q, me).start())
        whole(parts.at[pl.ds(0, count - 1)], recv.at[0])
        whole(parts.at[pl.ds(0, count - 1)], send.at[0])
        total = parts[0]
        for j in range(1, count):
            total = total + parts[j]
        return total

    if together:
        row = reduced(row, nl * n, lat * n + prop, prop_parts, 1, prop_send, prop_recv, lambda j: at(j // n, j % n))
    else:
        row = reduced(row, nl, lat, lat_parts, 0, lat_send, lat_recv, lambda l: at(l, prop))
        row = reduced(row, n, prop, prop_parts, 1, prop_send, prop_recv, at_prop)
    wide = jnp.broadcast_to(row, (S, NY))
    cross_total = jnp.sum(jnp.where(on_cross, wide, 0.0), axis=1, keepdims=True)
    self_total = jnp.sum(jnp.where(on_self, wide, 0.0), axis=1, keepdims=True)
    size = jnp.broadcast_to(cross_total / (self_total + tiny), (S, NY))
    for c in range(2):
        for k in range(3):
            for z in range(Z):
                for x in range(X):
                    base = (c * 3 + k) * S * ZX + z * X + x
                    out_ref[pl.ds(base, S, stride=ZX), :] = field[c, k, z + 1, x + 1] + size * pre[c, k, z + 1, x + 1]
    for copy, out, _ in halos + sides:
        pl.when(out)(copy.wait_send)
    whole(corner_all.at[pl.ds(0, n - 1)], corner_send.at[0])
    whole(tips_in.at[pl.ds(0, (n - 1) * rows)], tips_send.at[0])
    whole(ends_in.at[pl.ds(0, (n - 1) * rows)], ends_send.at[0])


def per_device(n, nl, right_side, start_field, region, core_mask, intensity, eps_lin, eps_loss, kerr_coef):
    S, Z, X, NY = right_side.shape[2:]
    ns = n
    lo = (n - ns) // 2
    m = ns // X
    u = S // m
    rows = -(-12 * u // 8) * 8
    together = n * nl <= 64
    team = n * nl if together else n
    dims = (n, nl, S, Z, X, NY, ns, lo, u, m, rows, together)
    flat = (6 * S * Z * X, NY)
    f32 = jnp.float32
    vmem = pl.BlockSpec(memory_space=pltpu.VMEM)
    smem = pl.BlockSpec(memory_space=pltpu.SMEM)
    dma = pltpu.SemaphoreType.DMA
    new = pl.pallas_call(
        functools.partial(kernel, dims),
        out_shape=pltpu.VMEM(flat, f32),
        in_specs=[smem] * 3 + [pl.BlockSpec(memory_space=pltpu.HBM)] * 5,
        out_specs=vmem,
        scratch_shapes=[
            pltpu.VMEM(region.shape, region.dtype),
            pltpu.VMEM(region.shape, core_mask.dtype),
            pltpu.VMEM(region.shape, f32),
            pltpu.VMEM(flat, f32),
            pltpu.VMEM(flat, f32),
            dma((5,)),
            pltpu.SemaphoreType.REGULAR((n.bit_length() + nl.bit_length(),)),
            pltpu.VMEM((2, 3, Z + 2, X + 2, S, NY), f32),
            pltpu.VMEM((2, 3, Z, X, S, NY), f32),
            pltpu.VMEM((2, 3, Z, X, S, NY), f32),
            pltpu.VMEM((2, 3, Z + 2, X + 2, S, NY), f32),
            pltpu.VMEM((8, Z, X, 1, NY), f32),
            pltpu.VMEM((X, 8, NY), f32),
            pltpu.VMEM((n, 8, NY), f32),
            pltpu.VMEM((n, 10, 1, NY), f32),
            pltpu.VMEM((ns * rows, NY), f32),
            pltpu.VMEM((n * rows, NY), f32),
            pltpu.VMEM((n * rows, NY), f32),
            pltpu.VMEM((ns * rows, NY), f32),
            pltpu.VMEM((2, 1, NY), f32),
            pltpu.VMEM((nl, 1, NY), f32),
            pltpu.VMEM((team, 1, NY), f32),
            dma((6,)), dma((6,)),
            dma((n,)), dma((n,)),
            dma((n,)), dma((n,)),
            dma((n,)), dma((n,)),
            dma((2,)), dma((2,)),
            dma((nl,)), dma((nl,)),
            dma((team,)), dma((team,)),
        ],
        compiler_params=pltpu.CompilerParams(
            collective_id=0, has_side_effects=True, vmem_limit_bytes=60 * 1024 * 1024
        ),
    )(eps_lin, eps_loss, kerr_coef, region, core_mask, intensity, right_side.reshape(flat), start_field.reshape(flat))
    return new.reshape(right_side.shape)


def solution(mesh):
    placed = (
        P(None, None, None, "prop", "lat", None),
        P(None, None, None, "prop", "lat", None),
        P("prop", "lat", None),
        P("prop", "lat", None),
        P("prop", "lat", None),
        P(),
        P(),
        P(),
    )
    return jax.shard_map(
        functools.partial(per_device, mesh.shape["prop"], mesh.shape["lat"]),
        mesh=mesh,
        in_specs=placed,
        out_specs=P(None, None, None, "prop", "lat", None),
        check_vma=False,
    )
```
